32 devices in a mesh: group: 2 (over x), ctx: 16 (over z, y, core).
Axes of the slice: x: 2, y: 2, z: 4, core: 2. Of those that a mesh axis runs over, the one named last changes fastest.
Arguments:
- queries: bfloat16 [4, 1536, 1024], P('group', 'ctx'), parts along dimension 0, may hold values from -6 to 6
- keys: bfloat16 [4, 1536, 128], P('group', 'ctx'), parts along dimension 0, may hold values from -6 to 6
- values: bfloat16 [4, 1536, 128], P('group', 'ctx'), parts along dimension 0, may hold values from -6 to 6
- lengths: int32 [4], P('group'), parts along dimension 0, may hold values from 384 to 1536, as said below
Outputs:
- attended: bfloat16 [4, 1536, 1024], P('group', 'ctx'), parts along dimension 0
The draws below stay inside these ranges and needn't reach their ends.
There are 2 independent parts, one for each index of `group`. The reference program is written for one: setup_inputs(seed, part) draws one part's arguments, and reference() takes and returns one part's arrays. A program takes and returns all parts, laid end to end along the dimension named above; each array names one. Nothing has to cross between parts.
Inputs may be any that keep to these rules, and one draw needn't show every extreme that they name: `lengths`: in every draw at least one sequence has all 1536 positions real.
All inputs are finite; a program needn't handle non-finite values.
Results may differ from the reference program's by a relative error of at most 0.0045.
Values may be sent and summed in bfloat16 or wider, within the bound.
A program may use at most 64 MiB of HBM per device.

```python
import jax
import jax.numpy as jnp
from jax import lax

HD = 128
QH = 8
SEQS = 2
L = 1536


def base_field(key, shape):
    return jnp.clip(jax.random.normal(key, shape, jnp.float32), -6.0, 6.0)


def draw_queries(key, part):
    field = base_field(jax.random.fold_in(key, 1), (SEQS, L, QH * HD))
    return field.astype(jnp.bfloat16)


def draw_keys(key, part):
    field = base_field(jax.random.fold_in(key, 2), (SEQS, L, HD))
    return field.astype(jnp.bfloat16)


def draw_lengths(key, part):
    drawn = jax.random.randint(jax.random.fold_in(key, 3), (SEQS,), L // 4, L + 1)
    longest = jax.random.randint(jax.random.fold_in(key, 4), (), 0, SEQS)
    seq_ids = jnp.arange(SEQS, dtype=jnp.int32)
    drawn = jnp.where(seq_ids == longest, L, drawn)
    return drawn.astype(jnp.int32)


def levels(rng, dims, split, least, high):
    factor_of, own = 1.0, jax.random.fold_in(rng, 6)
    for axis_at, blocks in split:
        heights = jnp.exp(jax.random.uniform(jax.random.fold_in(own, axis_at), (blocks,), jnp.float32, least / len(split), high / len(split)))
        factor_of = factor_of * jnp.repeat(heights, dims[axis_at] // blocks).reshape([-1 if axis == axis_at else 1 for axis in range(len(dims))])
    return factor_of


def bell_draw(rng, shape, scale, most, shards=(), held_as=jnp.bfloat16):
    gain = levels(rng, shape, shards, -0.22, 0.18) if shards else 1.0
    values = jax.random.normal(rng, shape, jnp.float32) * scale * gain
    return jnp.minimum(jnp.maximum(values, -most), most).astype(held_as)


def setup_inputs(seed: int = 0, part: int = 0) -> dict:
    key_of = jax.random.split(jax.random.key(seed), 5)
    part_splits = jax.random.split(jax.random.fold_in(key_of[4], part), 5)
    return {
        "queries": draw_queries(jax.random.fold_in(jax.random.fold_in(key_of[4], part), 71), part),
        "keys": draw_keys(jax.random.fold_in(jax.random.fold_in(key_of[4], part), 71), part),
        "values": bell_draw(part_splits[2], (SEQS, L, HD), 1.0, 6.0, ((1, 16),)),
        "lengths": draw_lengths(jax.random.fold_in(jax.random.fold_in(key_of[4], part), 71), part),
    }


NEG_FILL = -1e30


def reference(queries, keys, values, lengths):
    score_scale = HD ** -0.5
    block_rows = 512
    results = []
    for seq_idx in range(SEQS):
        key_float = keys[seq_idx].astype(jnp.float32)
        value_float = values[seq_idx].astype(jnp.float32)
        seq_queries = queries[seq_idx]
        valid_len = lengths[seq_idx]

        def attend_block(blk_idx):
            first_row = blk_idx * block_rows
            query_blk = lax.dynamic_slice_in_dim(seq_queries, first_row, block_rows, 0)
            query_blk = query_blk.astype(jnp.float32).reshape(block_rows, QH, HD)
            scores = jnp.einsum("qhd,kd->hqk", query_blk, key_float) * score_scale
            query_pos = first_row + jnp.arange(block_rows, dtype=jnp.int32)
            key_pos = jnp.arange(L, dtype=jnp.int32)
            visible = (key_pos[None, :] <= query_pos[:, None]) & (key_pos[None, :] < valid_len)
            scores = jnp.where(visible[None], scores, NEG_FILL)
            row_max = jnp.max(scores, axis=-1)
            weights = jnp.where(visible[None], jnp.exp(scores - row_max[..., None]), 0.0)
            row_sum = jnp.sum(weights, axis=-1)
            rounded = lax.optimization_barrier(weights.astype(jnp.bfloat16)).astype(jnp.float32)
            numer_sum = jnp.einsum("hqk,kd->hqd", rounded, value_float)
            is_valid = query_pos < valid_len
            divisor = jnp.where(is_valid, row_sum, 1.0)
            result = jnp.where(is_valid[None, :, None], numer_sum / divisor[..., None], 0.0)
            return result.transpose(1, 0, 2).reshape(block_rows, QH * HD).astype(jnp.bfloat16)

        blocks = lax.map(attend_block, jnp.arange(L // block_rows, dtype=jnp.int32))
        results.append(blocks.reshape(L, QH * HD))
    return jnp.stack(results, axis=0)
```

```python
import functools
import math

import jax
import jax.numpy as jnp
from jax import lax
from jax.experimental import pallas as pl
from jax.experimental.pallas import tpu as pltpu
from jax.sharding import PartitionSpec as P

NEG_FILL = -1e30
MESH = pl.DeviceIdType.MESH
HEADS_PER_CHUNK = 4


def kernel(outer, mid, len_ref, q_hbm, k_hbm, v_hbm, o_ref, kv, qbuf, m_ref, l_ref, acc_ref,
           local_sem, recv_sem, send_z, send_y, send_c):
    seqs, heads, rows, hd = qbuf.shape
    plane = mid * 2
    group_keys = plane * rows
    scale2 = (hd ** -0.5) * math.log2(math.e)
    me = lax.axis_index("ctx")
    grp = lax.axis_index("group")
    core = lax.rem(me, 2)
    mine = lax.rem(me // 2, mid)
    o = me // plane

    def idx(oo, mm, cc):
        return (oo * mid + mm) * 2 + cc

    def peer(j):
        return lax.rem(mine + j, mid)

    def block(b):
        return kv.at[:, :, pl.ds(pl.multiple_of(b * rows, rows), rows), :]

    def rcopy(b, dev, sem):
        return pltpu.make_async_remote_copy(
            src_ref=block(b), dst_ref=block(b), send_sem=sem, recv_sem=recv_sem.at[b],
            device_id=(grp, dev), device_id_type=MESH)

    own = pl.ds(pl.multiple_of(me * rows, rows), rows)
    kv_loads = [
        pltpu.make_async_copy(k_hbm, kv.at[0, :, own, :], local_sem.at[0]),
        pltpu.make_async_copy(v_hbm, kv.at[1, :, own, :], local_sem.at[1]),
    ]
    q_loads = [
        pltpu.make_async_copy(q_hbm.at[:, :, pl.ds(h * hd, hd)], qbuf.at[:, h], local_sem.at[2 + h])
        for h in range(heads)
    ]
    for c in kv_loads:
        c.start()

    barrier = pltpu.get_barrier_semaphore()
    partner_core = idx(o, mine, 1 - core)

    def greet(dev):
        pl.semaphore_signal(barrier, inc=1, device_id=(grp, dev), device_id_type=MESH)

    for d in range(1, outer):
        greet(idx(lax.rem(o + d, outer), mine, core))
    for j in range(1, mid):
        greet(idx(o, peer(j), core))
    greet(partner_core)
    for c in q_loads:
        c.start()
    for c in kv_loads:
        c.wait()
    pl.semaphore_wait(barrier, outer - 1 + mid - 1 + 1)

    def forward(d):
        b = idx(o - d, mine, core)
        for j in range(1, mid):
            rcopy(b, idx(o, peer(j), core), send_y.at[d, j]).start()
        rcopy(b, partner_core, send_c.at[d, 0]).start()

    for d in range(1, outer):
        @pl.when(o + d < outer)
        def _():
            rcopy(me, idx(o + d, mine, core), send_z.at[d]).start()
    forward(0)

    m_ref[...] = jnp.full(m_ref.shape, NEG_FILL, jnp.float32)
    l_ref[...] = jnp.zeros(l_ref.shape, jnp.float32)
    acc_ref[...] = jnp.zeros(acc_ref.shape, jnp.float32)
    query_pos = me * rows + lax.broadcasted_iota(jnp.int32, (rows, group_keys), 0)
    key_off = lax.broadcasted_iota(jnp.int32, (rows, group_keys), 1)
    for c in q_loads:
        c.wait()

    def step(d, carry):
        for j in range(1, mid):
            b = idx(o - d, peer(j), core)
            rcopy(b, partner_core, send_c.at[d, j]).wait_recv()
            rcopy(b, partner_core, send_c.at[d, j]).start()

        @pl.when(d < o)
        def _():
            b = idx(o - d - 1, mine, core)
            rcopy(b, partner_core, send_c.at[d + 1, 0]).wait_recv()
            forward(d + 1)

        for j in range(mid):
            b = idx(o - d, peer(j), 1 - core)
            rcopy(b, partner_core, send_c.at[d, j]).wait_recv()

        first = pl.multiple_of((o - d) * group_keys, group_keys)
        keys_at = pl.ds(first, group_keys)
        hc = HEADS_PER_CHUNK
        for s in range(seqs):
            visible = (first + key_off <= query_pos) & (first + key_off < len_ref[s])
            bias = jnp.where(visible, 0.0, NEG_FILL)
            k_blk = kv[0, s, keys_at, :]
            v_blk = kv[1, s, keys_at, :]
            for h in range(0, heads, hc):
                q_blk = qbuf[s, h:h + hc].reshape(hc * rows, hd)
                sc = lax.dot_general(q_blk, k_blk, (((1,), (1,)), ((), ())),
                                     preferred_element_type=jnp.float32)
                sc = sc.reshape(hc, rows, group_keys) + bias[None]
                m_old = m_ref[s, h:h + hc]
                m_new = jnp.maximum(m_old, jnp.max(sc, axis=-1, keepdims=True))
                m_ref[s, h:h + hc] = m_new
                p = jnp.exp2((sc - m_new[:, :, :1]) * scale2)
                alpha = jnp.exp2((m_old - m_new) * scale2)
                part = p[:, :, :hd]
                for t in range(hd, group_keys, hd):
                    part = part + p[:, :, t:t + hd]
                l_ref[s, h:h + hc] = l_ref[s, h:h + hc] * alpha + part
                pv = jnp.dot(p.astype(jnp.bfloat16).reshape(hc * rows, group_keys), v_blk,
                             preferred_element_type=jnp.float32)
                acc_ref[s, h:h + hc] = acc_ref[s, h:h + hc] * alpha + pv.reshape(hc, rows, hd)
        return carry

    lax.fori_loop(0, o + 1, step, jnp.int32(0))

    pos = me * rows + lax.broadcasted_iota(jnp.int32, (rows, hd), 0)
    for s in range(seqs):
        is_valid = pos < len_ref[s]
        for h in range(heads):
            total = jnp.sum(l_ref[s, h], axis=-1, keepdims=True)
            divisor = jnp.where(is_valid, total, 1.0)
            res = jnp.where(is_valid, acc_ref[s, h] / divisor, 0.0)
            o_ref[s, :, h * hd:(h + 1) * hd] = res.astype(jnp.bfloat16)

    for d in range(1, outer):
        @pl.when(o + d < outer)
        def _():
            rcopy(me, idx(o + d, mine, core), send_z.at[d]).wait_send()

    def drain(d, carry):
        b = idx(o - d, mine, core)
        for j in range(1, mid):
            rcopy(b, partner_core, send_y.at[d, j]).wait_send()
        for j in range(mid):
            rcopy(b, partner_core, send_c.at[d, j]).wait_send()
        return carry

    lax.fori_loop(0, o + 1, drain, jnp.int32(0))


def solution(mesh):
    n = mesh.shape["ctx"]
    mid = 1
    while mid * mid * 4 * 2 <= n:
        mid *= 2
    outer = n // (2 * mid)

    def local(queries, keys, values, lengths):
        seqs, rows, width = queries.shape
        hd = keys.shape[2]
        heads = width // hd
        hbm = pl.BlockSpec(memory_space=pl.ANY)
        return pl.pallas_call(
            functools.partial(kernel, outer, mid),
            out_shape=jax.ShapeDtypeStruct(queries.shape, jnp.bfloat16),
            in_specs=[pl.BlockSpec(memory_space=pltpu.SMEM), hbm, hbm, hbm],
            out_specs=pl.BlockSpec(memory_space=pltpu.VMEM),
            scratch_shapes=[
                pltpu.VMEM((2, seqs, n * rows, hd), jnp.bfloat16),
                pltpu.VMEM((seqs, heads, rows, hd), jnp.bfloat16),
                pltpu.VMEM((seqs, heads, rows, hd), jnp.float32),
                pltpu.VMEM((seqs, heads, rows, hd), jnp.float32),
                pltpu.VMEM((seqs, heads, rows, hd), jnp.float32),
                pltpu.SemaphoreType.DMA((2 + heads,)),
                pltpu.SemaphoreType.DMA((n,)),
                pltpu.SemaphoreType.DMA((outer,)),
                pltpu.SemaphoreType.DMA((outer, mid)),
                pltpu.SemaphoreType.DMA((outer, mid)),
            ],
            compiler_params=pltpu.CompilerParams(
                collective_id=0, has_side_effects=True, vmem_limit_bytes=48 * 1024 * 1024),
        )(lengths, queries, keys, values)

    return jax.shard_map(
        local, mesh=mesh,
        in_specs=(P("group", "ctx", None), P("group", "ctx", None), P("group", "ctx", None), P("group")),
        out_specs=P("group", "ctx", None), check_vma=False)
```

```python
import functools
import math

import jax
import jax.numpy as jnp
from jax import lax
from jax.experimental import pallas as pl
from jax.experimental.pallas import tpu as pltpu
from jax.sharding import PartitionSpec as P

NEG_FILL = -1e30
MESH = pl.DeviceIdType.MESH
HEADS_PER_CHUNK = 8


def kernel(outer, mid, len_hbm, q_hbm, k_hbm, v_hbm, o_ref, kv, qbuf, m_ref, l_ref, acc_ref, len_ref,
           local_sem, recv_sem, send_z, send_y, send_c):
    seqs, heads, rows, hd = qbuf.shape
    plane = mid * 2
    group_keys = plane * rows
    scale2 = (hd ** -0.5) * math.log2(math.e)
    me = lax.axis_index("ctx")
    grp = lax.axis_index("group")
    core = lax.rem(me, 2)
    mine = lax.rem(me // 2, mid)
    o = me // plane

    def idx(oo, mm, cc):
        return (oo * mid + mm) * 2 + cc

    def peer(j):
        return lax.rem(mine + j, mid)

    def unit(b, s):
        return kv.at[:, s, pl.ds(pl.multiple_of(b * rows, rows), rows), :]

    def rcopy(b, s, dev, sem):
        return pltpu.make_async_remote_copy(
            src_ref=unit(b, s), dst_ref=unit(b, s), send_sem=sem, recv_sem=recv_sem.at[b, s],
            device_id=(grp, dev), device_id_type=MESH)

    own = pl.ds(pl.multiple_of(me * rows, rows), rows)
    kv_loads = [
        pltpu.make_async_copy(k_hbm, kv.at[0, :, own, :], local_sem.at[0]),
        pltpu.make_async_copy(v_hbm, kv.at[1, :, own, :], local_sem.at[1]),
    ]
    q_loads = [
        pltpu.make_async_copy(q_hbm.at[:, :, pl.ds(h * hd, hd)], qbuf.at[:, h], local_sem.at[2 + h])
        for h in range(heads)
    ]
    len_load = pltpu.make_async_copy(len_hbm, len_ref, local_sem.at[2 + heads])
    for c in kv_loads:
        c.start()
    len_load.start()

    barrier = pltpu.get_barrier_semaphore()
    partner_core = idx(o, mine, 1 - core)

    def greet(dev):
        pl.semaphore_signal(barrier, inc=1, device_id=(grp, dev), device_id_type=MESH)

    has_up = o < outer - 1
    has_down = o > 0
    above = idx(jnp.minimum(o + 1, outer - 1), mine, core)
    below = idx(jnp.maximum(o - 1, 0), mine, core)

    @pl.when(has_up)
    def _():
        greet(above)

    @pl.when(has_down)
    def _():
        greet(below)

    for j in range(1, mid):
        greet(idx(o, peer(j), core))
    greet(partner_core)
    for c in q_loads:
        c.start()
    for c in kv_loads:
        c.wait()
    pl.semaphore_wait(barrier, mid + has_up.astype(jnp.int32) + has_down.astype(jnp.int32))

    def forward(u):
        d, s = u // seqs, lax.rem(u, seqs)
        b = idx(o - d, mine, core)

        @pl.when(has_up)
        def _():
            rcopy(b, s, above, send_z.at[u]).start()

        for j in range(1, mid):
            rcopy(b, s, idx(o, peer(j), core), send_y.at[u, j]).start()
        rcopy(b, s, partner_core, send_c.at[u, 0]).start()

    for u in range(seqs):
        forward(u)

    m_ref[...] = jnp.full(m_ref.shape, NEG_FILL, jnp.float32)
    l_ref[...] = jnp.zeros(l_ref.shape, jnp.float32)
    acc_ref[...] = jnp.zeros(acc_ref.shape, jnp.float32)
    query_pos = me * rows + lax.broadcasted_iota(jnp.int32, (rows, group_keys), 0)
    key_off = lax.broadcasted_iota(jnp.int32, (rows, group_keys), 1)
    for c in q_loads:
        c.wait()
    len_load.wait()

    def attend(u):
        d, s = u // seqs, lax.rem(u, seqs)
        for j in range(mid):
            rcopy(idx(o - d, peer(j), 1 - core), s, partner_core, send_c.at[u, j]).wait_recv()
        first = pl.multiple_of((o - d) * group_keys, group_keys)
        keys_at = pl.ds(first, group_keys)
        hc = HEADS_PER_CHUNK
        visible = (first + key_off <= query_pos) & (first + key_off < len_ref[s])
        bias = jnp.where(visible, 0.0, NEG_FILL)
        k_blk = kv[0, s, keys_at, :]
        v_blk = kv[1, s, keys_at, :]
        for h in range(0, heads, hc):
            hs = pl.ds(h, hc)
            q_blk = qbuf[s, hs].reshape(hc * rows, hd)
            sc = lax.dot_general(q_blk, k_blk, (((1,), (1,)), ((), ())),
                                 preferred_element_type=jnp.float32)
            sc = sc.reshape(hc, rows, group_keys) + bias[None]
            m_old = m_ref[s, hs]
            m_new = jnp.maximum(m_old, jnp.max(sc, axis=-1, keepdims=True))
            m_ref[s, hs] = m_new
            p = jnp.exp2((sc - m_new[:, :, :1]) * scale2)
            alpha = jnp.exp2((m_old - m_new) * scale2)
            part = p[:, :, :hd]
            for t in range(hd, group_keys, hd):
                part = part + p[:, :, t:t + hd]
            l_ref[s, hs] = l_ref[s, hs] * alpha + part
            pv = jnp.dot(p.astype(jnp.bfloat16).reshape(hc * rows, group_keys), v_blk,
                         preferred_element_type=jnp.float32)
            acc_ref[s, hs] = acc_ref[s, hs] * alpha + pv.reshape(hc, rows, hd)

    units = (o + 1) * seqs

    def step(u, carry):
        @pl.when(u + seqs < units)
        def _():
            w = u + seqs
            rcopy(idx(o - w // seqs, mine, core), lax.rem(w, seqs), partner_core,
                  send_c.at[w, 0]).wait_recv()
            forward(w)

        @pl.when(u < units)
        def _():
            for j in range(1, mid):
                b, s = idx(o - u // seqs, peer(j), core), lax.rem(u, seqs)
                rcopy(b, s, partner_core, send_c.at[u, j]).wait_recv()
                rcopy(b, s, partner_core, send_c.at[u, j]).start()

        @pl.when(u > 0)
        def _():
            attend(u - 1)

        return carry

    lax.fori_loop(0, units + 1, step, jnp.int32(0))

    pos = me * rows + lax.broadcasted_iota(jnp.int32, (rows, hd), 0)
    for s in range(seqs):
        is_valid = pos < len_ref[s]
        for h in range(heads):
            total = jnp.sum(l_ref[s, h], axis=-1, keepdims=True)
            divisor = jnp.where(is_valid, total, 1.0)
            res = jnp.where(is_valid, acc_ref[s, h] / divisor, 0.0)
            o_ref[s, :, h * hd:(h + 1) * hd] = res.astype(jnp.bfloat16)

    def drain(u, carry):
        b, s = idx(o - u // seqs, mine, core), lax.rem(u, seqs)

        @pl.when(has_up)
        def _():
            rcopy(b, s, above, send_z.at[u]).wait_send()

        for j in range(1, mid):
            rcopy(b, s, partner_core, send_y.at[u, j]).wait_send()
        for j in range(mid):
            rcopy(b, s, partner_core, send_c.at[u, j]).wait_send()
        return carry

    lax.fori_loop(0, units, drain, jnp.int32(0))


def solution(mesh):
    n = mesh.shape["ctx"]
    mid = 1
    while mid * mid * 4 * 2 <= n:
        mid *= 2
    outer = n // (2 * mid)

    def local(queries, keys, values, lengths):
        seqs, rows, width = queries.shape
        hd = keys.shape[2]
        heads = width // hd
        queries, keys, values, lengths = (
            pltpu.with_memory_space_constraint(x, pltpu.HBM) for x in (queries, keys, values, lengths))
        hbm = pl.BlockSpec(memory_space=pltpu.HBM)
        return pl.pallas_call(
            functools.partial(kernel, outer, mid),
            out_shape=jax.ShapeDtypeStruct(queries.shape, jnp.bfloat16),
            in_specs=[hbm, hbm, hbm, hbm],
            out_specs=pl.BlockSpec(memory_space=pltpu.VMEM),
            scratch_shapes=[
                pltpu.VMEM((2, seqs, n * rows, hd), jnp.bfloat16),
                pltpu.VMEM((seqs, heads, rows, hd), jnp.bfloat16),
                pltpu.VMEM((seqs, heads, rows, hd), jnp.float32),
                pltpu.VMEM((seqs, heads, rows, hd), jnp.float32),
                pltpu.VMEM((seqs, heads, rows, hd), jnp.float32),
                pltpu.SMEM((seqs,), jnp.int32),
                pltpu.SemaphoreType.DMA((3 + heads,)),
                pltpu.SemaphoreType.DMA((n, seqs)),
                pltpu.SemaphoreType.DMA((outer * seqs,)),
                pltpu.SemaphoreType.DMA((outer * seqs, mid)),
                pltpu.SemaphoreType.DMA((outer * seqs, mid)),
            ],
            compiler_params=pltpu.CompilerParams(
                collective_id=0, has_side_effects=True, vmem_limit_bytes=48 * 1024 * 1024),
        )(lengths, queries, keys, values)

    return jax.shard_map(
        local, mesh=mesh,
        in_specs=(P("group", "ctx", None), P("group", "ctx", None), P("group", "ctx", None), P("group")),
        out_specs=P("group", "ctx", None), check_vma=False)
```

```python
import functools
import math

import jax
import jax.numpy as jnp
from jax import lax
from jax.experimental import pallas as pl
from jax.experimental.pallas import tpu as pltpu
from jax.sharding import PartitionSpec as P

NEG_FILL = -1e30
MESH = pl.DeviceIdType.MESH
HEADS_PER_CHUNK = 8


def kernel(outer, mid, len_hbm, q_hbm, k_hbm, v_hbm, o_ref, kv, qbuf, m_ref, l_ref, acc_ref, len_ref,
           local_sem, recv_sem, send_z, send_y, send_c, send_x):
    seqs, heads, rows, hd = qbuf.shape
    plane = mid * 2
    group_keys = plane * rows
    scale2 = (hd ** -0.5) * math.log2(math.e)
    me = lax.axis_index("ctx")
    grp = lax.axis_index("group")
    core = lax.rem(me, 2)
    mine = lax.rem(me // 2, mid)
    o = me // plane

    def idx(oo, mm, cc):
        return (oo * mid + mm) * 2 + cc

    def peer(j):
        return lax.rem(mine + j, mid)

    def unit(b, s):
        return kv.at[:, s, pl.ds(pl.multiple_of(b * rows, rows), rows), :]

    def rcopy(b, s, dev, sem):
        return pltpu.make_async_remote_copy(
            src_ref=unit(b, s), dst_ref=unit(b, s), send_sem=sem, recv_sem=recv_sem.at[b, s],
            device_id=(grp, dev), device_id_type=MESH)

    own = pl.ds(pl.multiple_of(me * rows, rows), rows)
    kv_loads = [
        pltpu.make_async_copy(k_hbm, kv.at[0, :, own, :], local_sem.at[0]),
        pltpu.make_async_copy(v_hbm, kv.at[1, :, own, :], local_sem.at[1]),
    ]
    q_loads = [
        pltpu.make_async_copy(q_hbm.at[:, :, pl.ds(h * hd, hd)], qbuf.at[:, h], local_sem.at[2 + h])
        for h in range(heads)
    ]
    len_load = pltpu.make_async_copy(len_hbm, len_ref, local_sem.at[2 + heads])
    for c in kv_loads:
        c.start()
    len_load.start()

    barrier = pltpu.get_barrier_semaphore()
    partner_core = idx(o, mine, 1 - core)

    def greet(dev):
        pl.semaphore_signal(barrier, inc=1, device_id=(grp, dev), device_id_type=MESH)

    has_up = o < outer - 1
    has_down = o > 0
    above = idx(jnp.minimum(o + 1, outer - 1), mine, core)
    below = idx(jnp.maximum(o - 1, 0), mine, core)

    @pl.when(has_up)
    def _():
        greet(above)

    @pl.when(has_down)
    def _():
        greet(below)

    for j in range(1, mid):
        greet(idx(o, peer(j), core))
    greet(partner_core)
    for c in q_loads:
        c.start()
    for c in kv_loads:
        c.wait()
    pl.semaphore_wait(barrier, mid + has_up.astype(jnp.int32) + has_down.astype(jnp.int32))

    units = (o + 1) * seqs

    def crosses(u, j):
        return (u < units - 1) | (o == 0) | (j != mid - 1)

    def forward(u):
        d, s = u // seqs, lax.rem(u, seqs)
        b = idx(o - d, mine, core)

        @pl.when(has_up)
        def _():
            rcopy(b, s, above, send_z.at[u]).start()

        for j in range(1, mid):
            @pl.when(crosses(u, j))
            def _():
                rcopy(b, s, idx(o, peer(j), core), send_y.at[u, j]).start()

        rcopy(b, s, partner_core, send_c.at[u, 0]).start()

    for u in range(seqs):
        forward(u)

    m_ref[...] = jnp.full(m_ref.shape, NEG_FILL, jnp.float32)
    l_ref[...] = jnp.zeros(l_ref.shape, jnp.float32)
    acc_ref[...] = jnp.zeros(acc_ref.shape, jnp.float32)
    query_pos = me * rows + lax.broadcasted_iota(jnp.int32, (rows, group_keys), 0)
    key_off = lax.broadcasted_iota(jnp.int32, (rows, group_keys), 1)
    for c in q_loads:
        c.wait()
    len_load.wait()

    def attend(u):
        d, s = u // seqs, lax.rem(u, seqs)
        for j in range(mid):
            rcopy(idx(o - d, peer(j), 1 - core), s, partner_core, send_c.at[u, j]).wait_recv()
        first = pl.multiple_of((o - d) * group_keys, group_keys)
        keys_at = pl.ds(first, group_keys)
        hc = HEADS_PER_CHUNK
        visible = (first + key_off <= query_pos) & (first + key_off < len_ref[s])
        bias = jnp.where(visible, 0.0, NEG_FILL)
        k_blk = kv[0, s, keys_at, :]
        v_blk = kv[1, s, keys_at, :]
        chunks = [pl.ds(h, hc) for h in range(0, heads, hc)]
        tiles = [slice(t, t + hd) for t in range(0, group_keys, hd)]
        state = [(m_ref[s, hs], l_ref[s, hs], acc_ref[s, hs]) for hs in chunks]
        scores = [
            lax.dot_general(qbuf[s, hs].reshape(hc * rows, hd), k_blk, (((1,), (1,)), ((), ())),
                            preferred_element_type=jnp.float32) for hs in chunks]
        done = []
        for sc, (m_old, l_old, acc_old) in zip(scores, state):
            sc = sc.reshape(hc, rows, group_keys)
            parts = [sc[:, :, t] + bias[None, :, t] for t in tiles]
            top = functools.reduce(jnp.maximum, parts)
            m_new = jnp.maximum(m_old, jnp.max(top, axis=-1, keepdims=True))
            parts = [jnp.exp2((x - m_new) * scale2) for x in parts]
            alpha = jnp.exp2((m_old - m_new) * scale2)
            l_new = l_old * alpha + functools.reduce(jnp.add, parts)
            p = jnp.concatenate([x.astype(jnp.bfloat16) for x in parts], axis=-1)
            pv = jnp.dot(p.reshape(hc * rows, group_keys), v_blk, preferred_element_type=jnp.float32)
            done.append((m_new, l_new, acc_old * alpha + pv.reshape(hc, rows, hd)))
        for hs, (m_new, l_new, acc_new) in zip(chunks, done):
            m_ref[s, hs] = m_new
            l_ref[s, hs] = l_new
            acc_ref[s, hs] = acc_new

    def step(u, carry):
        @pl.when(u + seqs < units)
        def _():
            w = u + seqs
            rcopy(idx(o - w // seqs, mine, core), lax.rem(w, seqs), partner_core,
                  send_c.at[w, 0]).wait_recv()
            forward(w)

        @pl.when(u < units)
        def _():
            for j in range(1, mid):
                b, s = idx(o - u // seqs, peer(j), core), lax.rem(u, seqs)
                rcopy(b, s, partner_core, send_c.at[u, j]).wait_recv()
                if j == 1:
                    @pl.when((u == units - 1) & has_up)
                    def _():
                        rcopy(b, s, above, send_x.at[0]).start()

                rcopy(b, s, partner_core, send_c.at[u, j]).start()

        @pl.when(u > 0)
        def _():
            attend(u - 1)

        return carry

    lax.fori_loop(0, units + 1, step, jnp.int32(0))

    pos = me * rows + lax.broadcasted_iota(jnp.int32, (rows, hd), 0)
    for s in range(seqs):
        is_valid = pos < len_ref[s]
        for h in range(heads):
            total = jnp.sum(l_ref[s, h], axis=-1, keepdims=True)
            divisor = jnp.where(is_valid, total, 1.0)
            res = jnp.where(is_valid, acc_ref[s, h] / divisor, 0.0)
            o_ref[s, :, h * hd:(h + 1) * hd] = res.astype(jnp.bfloat16)

    def drain(u, carry):
        b, s = idx(o - u // seqs, mine, core), lax.rem(u, seqs)

        @pl.when(has_up)
        def _():
            rcopy(b, s, above, send_z.at[u]).wait_send()

        for j in range(1, mid):
            @pl.when(crosses(u, j))
            def _():
                rcopy(b, s, partner_core, send_y.at[u, j]).wait_send()

        for j in range(mid):
            rcopy(b, s, partner_core, send_c.at[u, j]).wait_send()
        return carry

    lax.fori_loop(0, units, drain, jnp.int32(0))

    if mid > 1:
        @pl.when(has_up)
        def _():
            rcopy(idx(0, peer(1), core), seqs - 1, above, send_x.at[0]).wait_send()


def solution(mesh):
    n = mesh.shape["ctx"]
    mid = 1
    while mid * mid * 4 * 2 <= n:
        mid *= 2
    outer = n // (2 * mid)

    def local(queries, keys, values, lengths):
        seqs, rows, width = queries.shape
        hd = keys.shape[2]
        heads = width // hd
        queries, keys, values, lengths = (
            pltpu.with_memory_space_constraint(x, pltpu.HBM) for x in (queries, keys, values, lengths))
        hbm = pl.BlockSpec(memory_space=pltpu.HBM)
        return pl.pallas_call(
            functools.partial(kernel, outer, mid),
            out_shape=jax.ShapeDtypeStruct(queries.shape, jnp.bfloat16),
            in_specs=[hbm, hbm, hbm, hbm],
            out_specs=pl.BlockSpec(memory_space=pltpu.VMEM),
            scratch_shapes=[
                pltpu.VMEM((2, seqs, n * rows, hd), jnp.bfloat16),
                pltpu.VMEM((seqs, heads, rows, hd), jnp.bfloat16),
                pltpu.VMEM((seqs, heads, rows, hd), jnp.float32),
                pltpu.VMEM((seqs, heads, rows, hd), jnp.float32),
                pltpu.VMEM((seqs, heads, rows, hd), jnp.float32),
                pltpu.SMEM((seqs,), jnp.int32),
                pltpu.SemaphoreType.DMA((3 + heads,)),
                pltpu.SemaphoreType.DMA((n, seqs)),
                pltpu.SemaphoreType.DMA((outer * seqs,)),
                pltpu.SemaphoreType.DMA((outer * seqs, mid)),
                pltpu.SemaphoreType.DMA((outer * seqs, mid)),
                pltpu.SemaphoreType.DMA((1,)),
            ],
            compiler_params=pltpu.CompilerParams(
                collective_id=0, has_side_effects=True, vmem_limit_bytes=48 * 1024 * 1024),
        )(lengths, queries, keys, values)

    return jax.shard_map(
        local, mesh=mesh,
        in_specs=(P("group", "ctx", None), P("group", "ctx", None), P("group", "ctx", None), P("group")),
        out_specs=P("group", "ctx", None), check_vma=False)
```

```python
import functools
import math

import jax
import jax.numpy as jnp
from jax import lax
from jax.experimental import pallas as pl
from jax.experimental.pallas import tpu as pltpu
from jax.sharding import PartitionSpec as P

NEG_FILL = -1e30
MESH = pl.DeviceIdType.MESH
HEADS_PER_CHUNK = 8
RELAY_LAG = 2


def kernel(outer, mid, len_hbm, q_hbm, k_hbm, v_hbm, o_ref, kv, qbuf, m_ref, l_ref, acc_ref, len_ref,
           local_sem, recv_sem, send_z, send_y, send_c, send_x):
    seqs, heads, rows, hd = qbuf.shape
    plane = mid * 2
    group_keys = plane * rows
    scale2 = (hd ** -0.5) * math.log2(math.e)
    me = lax.axis_index("ctx")
    grp = lax.axis_index("group")
    core = lax.rem(me, 2)
    mine = lax.rem(me // 2, mid)
    o = me // plane

    def idx(oo, mm, cc):
        return (oo * mid + mm) * 2 + cc

    def peer(j):
        return lax.rem(mine + j, mid)

    def unit(b, s):
        return kv.at[:, s, pl.ds(pl.multiple_of(b * rows, rows), rows), :]

    def rcopy(b, s, dev, sem):
        return pltpu.make_async_remote_copy(
            src_ref=unit(b, s), dst_ref=unit(b, s), send_sem=sem, recv_sem=recv_sem.at[b, s],
            device_id=(grp, dev), device_id_type=MESH)

    own = pl.ds(pl.multiple_of(me * rows, rows), rows)
    kv_loads = [
        pltpu.make_async_copy(k_hbm, kv.at[0, :, own, :], local_sem.at[0]),
        pltpu.make_async_copy(v_hbm, kv.at[1, :, own, :], local_sem.at[1]),
    ]
    q_loads = [
        pltpu.make_async_copy(q_hbm.at[:, :, pl.ds(h * hd, hd)], qbuf.at[:, h], local_sem.at[2 + h])
        for h in range(heads)
    ]
    len_load = pltpu.make_async_copy(len_hbm, len_ref, local_sem.at[2 + heads])
    for c in kv_loads:
        c.start()
    len_load.start()

    barrier = pltpu.get_barrier_semaphore()
    partner_core = idx(o, mine, 1 - core)

    def greet(dev):
        pl.semaphore_signal(barrier, inc=1, device_id=(grp, dev), device_id_type=MESH)

    has_up = o < outer - 1
    has_down = o > 0
    above = idx(jnp.minimum(o + 1, outer - 1), mine, core)
    below = idx(jnp.maximum(o - 1, 0), mine, core)

    @pl.when(has_up)
    def _():
        greet(above)

    @pl.when(has_down)
    def _():
        greet(below)

    for j in range(1, mid):
        greet(idx(o, peer(j), core))
    greet(partner_core)
    for c in q_loads:
        c.start()
    for c in kv_loads:
        c.wait()
    pl.semaphore_wait(barrier, mid + has_up.astype(jnp.int32) + has_down.astype(jnp.int32))

    units = (o + 1) * seqs

    def crosses(u, j):
        return (u < units - 1) | (o == 0) | (j != mid - 1)

    def forward(u):
        d, s = u // seqs, lax.rem(u, seqs)
        b = idx(o - d, mine, core)

        for j in range(1, mid):
            @pl.when(crosses(u, j))
            def _():
                rcopy(b, s, idx(o, peer(j), core), send_y.at[u, j]).start()

        rcopy(b, s, partner_core, send_c.at[u, 0]).start()

        @pl.when(has_up)
        def _():
            rcopy(b, s, above, send_z.at[u]).start()

    for u in range(seqs):
        forward(u)

    m_ref[...] = jnp.full(m_ref.shape, NEG_FILL, jnp.float32)
    l_ref[...] = jnp.zeros(l_ref.shape, jnp.float32)
    acc_ref[...] = jnp.zeros(acc_ref.shape, jnp.float32)
    query_pos = me * rows + lax.broadcasted_iota(jnp.int32, (rows, group_keys), 0)
    key_off = lax.broadcasted_iota(jnp.int32, (rows, group_keys), 1)
    for c in q_loads:
        c.wait()
    len_load.wait()

    def attend(u):
        d, s = u // seqs, lax.rem(u, seqs)
        for j in range(mid):
            rcopy(idx(o - d, peer(j), 1 - core), s, partner_core, send_c.at[u, j]).wait_recv()
        first = pl.multiple_of((o - d) * group_keys, group_keys)
        keys_at = pl.ds(first, group_keys)
        hc = HEADS_PER_CHUNK
        visible = (first + key_off <= query_pos) & (first + key_off < len_ref[s])
        bias = jnp.where(visible, 0.0, NEG_FILL)
        k_blk = kv[0, s, keys_at, :]
        v_blk = kv[1, s, keys_at, :]
        chunks = [pl.ds(h, hc) for h in range(0, heads, hc)]
        tiles = [slice(t, t + hd) for t in range(0, group_keys, hd)]
        state = [(m_ref[s, hs], l_ref[s, hs], acc_ref[s, hs]) for hs in chunks]
        scores = [
            lax.dot_general(qbuf[s, hs].reshape(hc * rows, hd), k_blk, (((1,), (1,)), ((), ())),
                            preferred_element_type=jnp.float32) for hs in chunks]
        done = []
        for sc, (m_old, l_old, acc_old) in zip(scores, state):
            sc = sc.reshape(hc, rows, group_keys)
            parts = [sc[:, :, t] + bias[None, :, t] for t in tiles]
            top = functools.reduce(jnp.maximum, parts)
            m_new = jnp.maximum(m_old, jnp.max(top, axis=-1, keepdims=True))
            parts = [jnp.exp2((x - m_new) * scale2) for x in parts]
            alpha = jnp.exp2((m_old - m_new) * scale2)
            l_new = l_old * alpha + functools.reduce(jnp.add, parts)
            p = jnp.concatenate([x.astype(jnp.bfloat16) for x in parts], axis=-1)
            pv = jnp.dot(p.reshape(hc * rows, group_keys), v_blk, preferred_element_type=jnp.float32)
            done.append((m_new, l_new, acc_old * alpha + pv.reshape(hc, rows, hd)))
        for hs, (m_new, l_new, acc_new) in zip(chunks, done):
            m_ref[s, hs] = m_new
            l_ref[s, hs] = l_new
            acc_ref[s, hs] = acc_new

    lag = jnp.where(has_up, RELAY_LAG, 1)

    def step(u, carry):
        @pl.when(u + seqs < units)
        def _():
            w = u + seqs
            rcopy(idx(o - w // seqs, mine, core), lax.rem(w, seqs), partner_core,
                  send_c.at[w, 0]).wait_recv()
            forward(w)

        @pl.when(u < units)
        def _():
            for j in range(1, mid):
                b, s = idx(o - u // seqs, peer(j), core), lax.rem(u, seqs)
                rcopy(b, s, partner_core, send_c.at[u, j]).wait_recv()
                if j == 1:
                    @pl.when((u == units - 1) & has_up)
                    def _():
                        rcopy(b, s, above, send_x.at[0]).start()

                rcopy(b, s, partner_core, send_c.at[u, j]).start()

        @pl.when(u >= lag)
        def _():
            attend(u - lag)

        return carry

    lax.fori_loop(0, units + lag, step, jnp.int32(0))

    pos = me * rows + lax.broadcasted_iota(jnp.int32, (rows, hd), 0)
    for s in range(seqs):
        is_valid = pos < len_ref[s]
        for h in range(heads):
            total = jnp.sum(l_ref[s, h], axis=-1, keepdims=True)
            divisor = jnp.where(is_valid, total, 1.0)
            res = jnp.where(is_valid, acc_ref[s, h] / divisor, 0.0)
            o_ref[s, :, h * hd:(h + 1) * hd] = res.astype(jnp.bfloat16)

    def drain(u, carry):
        b, s = idx(o - u // seqs, mine, core), lax.rem(u, seqs)

        @pl.when(has_up)
        def _():
            rcopy(b, s, above, send_z.at[u]).wait_send()

        for j in range(1, mid):
            @pl.when(crosses(u, j))
            def _():
                rcopy(b, s, partner_core, send_y.at[u, j]).wait_send()

        for j in range(mid):
            rcopy(b, s, partner_core, send_c.at[u, j]).wait_send()
        return carry

    lax.fori_loop(0, units, drain, jnp.int32(0))

    if mid > 1:
        @pl.when(has_up)
        def _():
            rcopy(idx(0, peer(1), core), seqs - 1, above, send_x.at[0]).wait_send()


def solution(mesh):
    n = mesh.shape["ctx"]
    mid = 1
    while mid * mid * 4 * 2 <= n:
        mid *= 2
    outer = n // (2 * mid)

    def local(queries, keys, values, lengths):
        seqs, rows, width = queries.shape
        hd = keys.shape[2]
        heads = width // hd
        queries, keys, values, lengths = (
            pltpu.with_memory_space_constraint(x, pltpu.HBM) for x in (queries, keys, values, lengths))
        hbm = pl.BlockSpec(memory_space=pltpu.HBM)
        return pl.pallas_call(
            functools.partial(kernel, outer, mid),
            out_shape=jax.ShapeDtypeStruct(queries.shape, jnp.bfloat16),
            in_specs=[hbm, hbm, hbm, hbm],
            out_specs=pl.BlockSpec(memory_space=pltpu.VMEM),
            scratch_shapes=[
                pltpu.VMEM((2, seqs, n * rows, hd), jnp.bfloat16),
                pltpu.VMEM((seqs, heads, rows, hd), jnp.bfloat16),
                pltpu.VMEM((seqs, heads, rows, hd), jnp.float32),
                pltpu.VMEM((seqs, heads, rows, hd), jnp.float32),
                pltpu.VMEM((seqs, heads, rows, hd), jnp.float32),
                pltpu.SMEM((seqs,), jnp.int32),
                pltpu.SemaphoreType.DMA((3 + heads,)),
                pltpu.SemaphoreType.DMA((n, seqs)),
                pltpu.SemaphoreType.DMA((outer * seqs,)),
                pltpu.SemaphoreType.DMA((outer * seqs, mid)),
                pltpu.SemaphoreType.DMA((outer * seqs, mid)),
                pltpu.SemaphoreType.DMA((1,)),
            ],
            compiler_params=pltpu.CompilerParams(
                collective_id=0, has_side_effects=True, vmem_limit_bytes=48 * 1024 * 1024),
        )(lengths, queries, keys, values)

    return jax.shard_map(
        local, mesh=mesh,
        in_specs=(P("group", "ctx", None), P("group", "ctx", None), P("group", "ctx", None), P("group")),
        out_specs=P("group", "ctx", None), check_vma=False)
```

```python
import functools
import math

import jax
import jax.numpy as jnp
from jax import lax
from jax.experimental import pallas as pl
from jax.experimental.pallas import tpu as pltpu
from jax.sharding import PartitionSpec as P

NEG_FILL = -1e30
MESH = pl.DeviceIdType.MESH
HEADS_PER_CHUNK = 8
RELAY_LAG = 2


def kernel(outer, mid, len_hbm, q_hbm, k_hbm, v_hbm, o_ref, kv, qbuf, m_ref, l_ref, acc_ref, len_ref,
           local_sem, recv_sem, send_z, send_y, send_c, send_x):
    seqs, heads, rows, hd = qbuf.shape
    plane = mid * 2
    group_keys = plane * rows
    scale2 = (hd ** -0.5) * math.log2(math.e)
    me = lax.axis_index("ctx")
    grp = lax.axis_index("group")
    core = lax.rem(me, 2)
    mine = lax.rem(me // 2, mid)
    o = me // plane

    def idx(oo, mm, cc):
        return (oo * mid + mm) * 2 + cc

    def peer(j):
        return lax.rem(mine + j, mid)

    def unit(b, s):
        return kv.at[:, s, pl.ds(pl.multiple_of(b * rows, rows), rows), :]

    def rcopy(b, s, dev, sem):
        return pltpu.make_async_remote_copy(
            src_ref=unit(b, s), dst_ref=unit(b, s), send_sem=sem, recv_sem=recv_sem.at[b, s],
            device_id=(grp, dev), device_id_type=MESH)

    own = pl.ds(pl.multiple_of(me * rows, rows), rows)
    kv_loads = [
        pltpu.make_async_copy(k_hbm, kv.at[0, :, own, :], local_sem.at[0]),
        pltpu.make_async_copy(v_hbm, kv.at[1, :, own, :], local_sem.at[1]),
    ]
    q_loads = [
        pltpu.make_async_copy(q_hbm.at[:, :, pl.ds(h * hd, hd)], qbuf.at[:, h], local_sem.at[2 + h])
        for h in range(heads)
    ]
    len_load = pltpu.make_async_copy(len_hbm, len_ref, local_sem.at[2 + heads])
    for c in kv_loads:
        c.start()
    len_load.start()

    barrier = pltpu.get_barrier_semaphore()
    partner_core = idx(o, mine, 1 - core)

    def greet(dev):
        pl.semaphore_signal(barrier, inc=1, device_id=(grp, dev), device_id_type=MESH)

    has_up = o < outer - 1
    has_down = o > 0
    above = idx(jnp.minimum(o + 1, outer - 1), mine, core)
    below = idx(jnp.maximum(o - 1, 0), mine, core)

    @pl.when(has_up)
    def _():
        greet(above)

    @pl.when(has_down)
    def _():
        greet(below)

    for j in range(1, mid):
        greet(idx(o, peer(j), core))
    greet(partner_core)
    for c in q_loads:
        c.start()
    for c in kv_loads:
        c.wait()
    pl.semaphore_wait(barrier, mid + has_up.astype(jnp.int32) + has_down.astype(jnp.int32))

    units = (o + 1) * seqs

    def crosses(u, j):
        return (u < units - 1) | (o == 0) | (j != mid - 1)

    def forward(u):
        d, s = u // seqs, lax.rem(u, seqs)
        b = idx(o - d, mine, core)

        for j in range(1, mid):
            @pl.when(crosses(u, j))
            def _():
                rcopy(b, s, idx(o, peer(j), core), send_y.at[u, j]).start()

        rcopy(b, s, partner_core, send_c.at[u, 0]).start()

        @pl.when(has_up)
        def _():
            rcopy(b, s, above, send_z.at[u]).start()

    for u in range(seqs):
        forward(u)

    m_ref[...] = jnp.full(m_ref.shape, NEG_FILL, jnp.float32)
    l_ref[...] = jnp.zeros(l_ref.shape, jnp.float32)
    acc_ref[...] = jnp.zeros(acc_ref.shape, jnp.float32)
    query_pos = me * rows + lax.broadcasted_iota(jnp.int32, (rows, group_keys), 0)
    key_off = lax.broadcasted_iota(jnp.int32, (rows, group_keys), 1)
    for c in q_loads:
        c.wait()
    len_load.wait()

    def attend(u):
        d, s = u // seqs, lax.rem(u, seqs)
        for j in range(mid):
            rcopy(idx(o - d, peer(j), 1 - core), s, partner_core, send_c.at[u, j]).wait_recv()
        first = pl.multiple_of((o - d) * group_keys, group_keys)
        keys_at = pl.ds(first, group_keys)
        hc = HEADS_PER_CHUNK
        visible = (first + key_off <= query_pos) & (first + key_off < len_ref[s])
        bias = jnp.where(visible, 0.0, NEG_FILL)
        k_blk = kv[0, s, keys_at, :]
        v_blk = kv[1, s, keys_at, :]
        chunks = [pl.ds(h, hc) for h in range(0, heads, hc)]
        tiles = [slice(t, t + hd) for t in range(0, group_keys, hd)]
        state = [(m_ref[s, hs], l_ref[s, hs], acc_ref[s, hs]) for hs in chunks]
        scores = [
            lax.dot_general(qbuf[s, hs].reshape(hc * rows, hd), k_blk, (((1,), (1,)), ((), ())),
                            preferred_element_type=jnp.float32) for hs in chunks]
        done = []
        for sc, (m_old, l_old, acc_old) in zip(scores, state):
            sc = sc.reshape(hc, rows, group_keys)
            parts = [sc[:, :, t] + bias[None, :, t] for t in tiles]
            top = functools.reduce(jnp.maximum, parts)
            m_new = jnp.maximum(m_old, jnp.max(top, axis=-1, keepdims=True))
            parts = [jnp.exp2((x - m_new) * scale2) for x in parts]
            alpha = jnp.exp2((m_old - m_new) * scale2)
            l_new = l_old * alpha + functools.reduce(jnp.add, parts)
            p = jnp.concatenate([x.astype(jnp.bfloat16) for x in parts], axis=-1)
            pv = jnp.dot(p.reshape(hc * rows, group_keys), v_blk, preferred_element_type=jnp.float32)
            done.append((m_new, l_new, acc_old * alpha + pv.reshape(hc, rows, hd)))
        for hs, (m_new, l_new, acc_new) in zip(chunks, done):
            m_ref[s, hs] = m_new
            l_ref[s, hs] = l_new
            acc_ref[s, hs] = acc_new

    lag = jnp.where(has_up, jnp.where(o == 0, 1, RELAY_LAG), 1)

    def step(u, carry):
        @pl.when(u + seqs < units)
        def _():
            w = u + seqs
            rcopy(idx(o - w // seqs, mine, core), lax.rem(w, seqs), partner_core,
                  send_c.at[w, 0]).wait_recv()
            forward(w)

        @pl.when(u < units)
        def _():
            for j in range(1, mid):
                b, s = idx(o - u // seqs, peer(j), core), lax.rem(u, seqs)
                rcopy(b, s, partner_core, send_c.at[u, j]).wait_recv()
                if j == 1:
                    @pl.when((u == units - 1) & has_up)
                    def _():
                        rcopy(b, s, above, send_x.at[0]).start()

                rcopy(b, s, partner_core, send_c.at[u, j]).start()

        @pl.when(u >= lag)
        def _():
            attend(u - lag)

        return carry

    lax.fori_loop(0, units + lag, step, jnp.int32(0))

    pos = me * rows + lax.broadcasted_iota(jnp.int32, (rows, hd), 0)
    for s in range(seqs):
        is_valid = pos < len_ref[s]
        for h in range(heads):
            total = jnp.sum(l_ref[s, h], axis=-1, keepdims=True)
            divisor = jnp.where(is_valid, total, 1.0)
            res = jnp.where(is_valid, acc_ref[s, h] / divisor, 0.0)
            o_ref[s, :, h * hd:(h + 1) * hd] = res.astype(jnp.bfloat16)

    def drain(u, carry):
        b, s = idx(o - u // seqs, mine, core), lax.rem(u, seqs)

        @pl.when(has_up)
        def _():
            rcopy(b, s, above, send_z.at[u]).wait_send()

        for j in range(1, mid):
            @pl.when(crosses(u, j))
            def _():
                rcopy(b, s, partner_core, send_y.at[u, j]).wait_send()

        for j in range(mid):
            rcopy(b, s, partner_core, send_c.at[u, j]).wait_send()
        return carry

    lax.fori_loop(0, units, drain, jnp.int32(0))

    if mid > 1:
        @pl.when(has_up)
        def _():
            rcopy(idx(0, peer(1), core), seqs - 1, above, send_x.at[0]).wait_send()


def solution(mesh):
    n = mesh.shape["ctx"]
    mid = 1
    while mid * mid * 4 * 2 <= n:
        mid *= 2
    outer = n // (2 * mid)

    def local(queries, keys, values, lengths):
        seqs, rows, width = queries.shape
        hd = keys.shape[2]
        heads = width // hd
        queries, keys, values, lengths = (
            pltpu.with_memory_space_constraint(x, pltpu.HBM) for x in (queries, keys, values, lengths))
        hbm = pl.BlockSpec(memory_space=pltpu.HBM)
        return pl.pallas_call(
            functools.partial(kernel, outer, mid),
            out_shape=jax.ShapeDtypeStruct(queries.shape, jnp.bfloat16),
            in_specs=[hbm, hbm, hbm, hbm],
            out_specs=pl.BlockSpec(memory_space=pltpu.VMEM),
            scratch_shapes=[
                pltpu.VMEM((2, seqs, n * rows, hd), jnp.bfloat16),
                pltpu.VMEM((seqs, heads, rows, hd), jnp.bfloat16),
                pltpu.VMEM((seqs, heads, rows, hd), jnp.float32),
                pltpu.VMEM((seqs, heads, rows, hd), jnp.float32),
                pltpu.VMEM((seqs, heads, rows, hd), jnp.float32),
                pltpu.SMEM((seqs,), jnp.int32),
                pltpu.SemaphoreType.DMA((3 + heads,)),
                pltpu.SemaphoreType.DMA((n, seqs)),
                pltpu.SemaphoreType.DMA((outer * seqs,)),
                pltpu.SemaphoreType.DMA((outer * seqs, mid)),
                pltpu.SemaphoreType.DMA((outer * seqs, mid)),
                pltpu.SemaphoreType.DMA((1,)),
            ],
            compiler_params=pltpu.CompilerParams(
                collective_id=0, has_side_effects=True, vmem_limit_bytes=48 * 1024 * 1024),
        )(lengths, queries, keys, values)

    return jax.shard_map(
        local, mesh=mesh,
        in_specs=(P("group", "ctx", None), P("group", "ctx", None), P("group", "ctx", None), P("group")),
        out_specs=P("group", "ctx", None), check_vma=False)
```
